32 devices in a mesh: grp: 2 (over x), tm: 16 (over z, y, core).
Axes of the slice: x: 2, y: 2, z: 4, core: 2. Of those that a mesh axis runs over, the one named last changes fastest.
Arguments:
- queries: bfloat16 [2, 8192, 1120], P(None, ('grp', 'tm')), parts along dimension 1, may hold values from 0.19921875 to 3
- keys: bfloat16 [2, 8192, 1120], P(None, ('grp', 'tm')), parts along dimension 1, may hold values from 0.05 to 24
- values: bfloat16 [2, 8192, 1120], P(None, ('grp', 'tm')), parts along dimension 1, may hold values from -12 to 12
- timesteps: int32 [4], P('grp'), parts along dimension 0, may hold values from 0 to 19
- gate_table: float32 [20, 2240], replicated, may hold values from -3 to 3
- out_weight: bfloat16 [1120, 2240], replicated, may hold values from -0.1875 to 0.1875
- conv_weight: float32 [9, 1120], replicated, may hold values from -1.5 to 1.5
Outputs:
- update: float32 [2, 8192, 2240], P(None, ('grp', 'tm')), parts along dimension 1
- fresh_state: float32 [32, 70, 70], P('grp'), parts along dimension 0
- fresh_total: float32 [32, 70], P('grp'), parts along dimension 0
The draws below stay inside these ranges and needn't reach their ends.
There are 2 independent parts, one for each index of `grp`. The reference program is written for one: setup_inputs(seed, part) draws one part's arguments, and reference() takes and returns one part's arrays. A program takes and returns all parts, laid end to end along the dimension named above; an argument that names none is the same for every part. Nothing has to cross between parts.
All inputs are finite; a program needn't handle non-finite values.
Results may differ from the reference program's by a relative error of at most 0.0003.
The reference program's roundings to bfloat16 on the way count: a program that leaves them out, or rounds other values in their place, can miss the bound.
Values may be sent and summed in bfloat16 or wider, within the bound.
A program may use at most 64 MiB of HBM per device.

```python
import math
import jax
import jax.numpy as jnp
from jax import lax

D = 2240
NH = 16
HD = 70
COLS = 64
NSTEPS = 20
ROWS_DEV = 4
FRAME_ROWS = 64
TOKENS = 4096
N_TM = 16


def both_fields(key):
    subkeys = jax.random.split(jax.random.fold_in(key, 11), 7)
    channels = NH * HD
    row_total = TOKENS // COLS
    row_ids = (jnp.arange(TOKENS, dtype=jnp.int32) // COLS).astype(jnp.float32)
    rise = (1.0 + 2.0 * row_ids / (row_total - 1.0))[:, None]
    log_keys = jax.random.uniform(subkeys[0], (TOKENS, channels), jnp.float32, -1.0, 1.0) + 0.5 * jax.random.normal(subkeys[1], (1, channels), jnp.float32)
    jitter = jax.random.normal(subkeys[2], (TOKENS, channels), jnp.float32)
    common = jax.random.normal(subkeys[3], (1, channels), jnp.float32)
    offsets = 0.7 * jax.random.normal(subkeys[4], (row_total, channels), jnp.float32)
    key_first = jnp.exp(log_keys) * rise
    key_second = key_first * jnp.exp(0.3 * jax.random.normal(subkeys[5], (TOKENS, channels), jnp.float32))
    value_first = jitter + common + jnp.repeat(offsets, COLS, axis=0)
    value_second = value_first + 0.5 * jax.random.normal(subkeys[6], (TOKENS, channels), jnp.float32)
    key_pair = jnp.clip(jnp.stack([key_first, key_second]), 0.05, 24.0)
    value_pair = jnp.clip(jnp.stack([value_first, value_second]), -12.0, 12.0)
    return (key_pair, value_pair)


def draw_keys(key, part):
    return both_fields(key)[0].astype(jnp.bfloat16)


def draw_values(key, part):
    return both_fields(key)[1].astype(jnp.bfloat16)


def shard_levels(rng, shape, cuts, smallest, high):
    def one(dim, shards_of):
        draws = jax.random.uniform(jax.random.fold_in(jax.random.fold_in(rng, 6), dim), (shards_of,), jnp.float32, smallest / len(cuts), high / len(cuts))
        return jnp.repeat(jnp.exp(draws), shape[dim] // shards_of).reshape((-1,) + (1,) * (len(shape) - dim - 1))

    gain = one(*cuts[0])
    for cut in cuts[1:]:
        gain = gain * one(*cut)
    return gain


def scatter_about(stream_key, shape, width, bound, held_as=jnp.bfloat16):
    return jnp.clip(width * jax.random.normal(stream_key, shape, jnp.float32), -bound, bound).astype(held_as)


def setup_inputs(seed: int = 0, part: int = 0) -> dict:
    streams_of = jax.random.split(jax.random.key(seed), 8)
    part_splits = jax.random.split(jax.random.fold_in(streams_of[7], part), 8)
    return {
        "queries": jnp.clip(jnp.exp(math.log(3.0) - 2.7119641 * jax.random.uniform(part_splits[0], (2, TOKENS, NH * HD), jnp.float32) ** shard_levels(part_splits[0], (2, TOKENS, NH * HD), ((1, 16),), -0.2, 0.2)), 0.19921875, 3.0).astype(jnp.bfloat16),
        "keys": draw_keys(jax.random.fold_in(jax.random.fold_in(streams_of[7], part), 71), part),
        "values": draw_values(jax.random.fold_in(jax.random.fold_in(streams_of[7], part), 71), part),
        "timesteps": jax.random.randint(part_splits[3], (2,), 0, NSTEPS).astype(jnp.int32),
        "gate_table": scatter_about(streams_of[4], (NSTEPS, D), 0.6, 3.0, jnp.float32),
        "out_weight": scatter_about(streams_of[5], (NH * HD, D), (NH * HD) ** -0.5, 0.1875),
        "conv_weight": scatter_about(streams_of[6], (9, NH * HD), 0.3, 1.5, jnp.float32),
    }


EXACT = lax.Precision.HIGHEST


def select_gate(gate_table, position):
    step_ids = jnp.arange(gate_table.shape[0], dtype=jnp.int32)
    return jnp.sum(jnp.where((step_ids == position)[:, None], gate_table, jnp.zeros_like(gate_table)), axis=0)


def shard_states(key_rows, values):
    key_grid = key_rows.astype(jnp.float32).reshape(N_TM, -1, NH, HD)
    value_grid = values.astype(jnp.float32).reshape(N_TM, -1, NH, HD)
    key_state = jnp.einsum('jrhd,jrhe->jhde', key_grid, value_grid, precision=EXACT)
    key_total = jnp.sum(key_grid, axis=1)
    return key_state, key_total


def spread(queries, key_state, key_total):
    query_grid = queries.astype(jnp.float32).reshape(N_TM, -1, NH, HD)
    numer = jnp.einsum('jrhd,jhde->jrhe', query_grid, key_state, precision=EXACT)
    denom = jnp.einsum('jrhd,jhd->jrh', query_grid, key_total, precision=EXACT)
    return (numer / denom[..., None]).reshape(-1, NH * HD)


def rim_rows(rims):
    per_frame = FRAME_ROWS // ROWS_DEV
    shard_ids = jnp.arange(N_TM, dtype=jnp.int32)
    upper_rim = jnp.concatenate([jnp.zeros_like(rims[:1, -1]), rims[:-1, -1]], axis=0)
    lower_rim = jnp.concatenate([rims[1:, 0], jnp.zeros_like(rims[:1, 0])], axis=0)
    upper_rim = jnp.where((shard_ids % per_frame != 0)[:, None, None], upper_rim, jnp.zeros_like(upper_rim))
    lower_rim = jnp.where(((shard_ids + 1) % per_frame != 0)[:, None, None], lower_rim, jnp.zeros_like(lower_rim))
    return upper_rim, lower_rim


def convolve(center, upper_rim, lower_rim, conv_weight):
    padded = jnp.concatenate([upper_rim[:, None], center, lower_rim[:, None]], axis=1).astype(jnp.float32)
    padded = jnp.pad(padded, ((0, 0), (0, 0), (1, 1), (0, 0)))
    summed = jnp.zeros(center.shape, jnp.float32)
    for tap_row in range(3):
        for tap_col in range(3):
            summed = summed + padded[:, tap_row:tap_row + ROWS_DEV, tap_col:tap_col + COLS] * conv_weight[3 * tap_row + tap_col]
    return summed.reshape(-1, center.shape[-1])


def reference(queries, keys, values, timesteps, gate_table, out_weight, conv_weight):
    channels = NH * HD
    gates = [select_gate(gate_table, timesteps[section]) for section in range(2)]
    state_one, total_one = shard_states(keys[0], values[0])
    state_two, total_two = shard_states(keys[1], values[1])
    whole_state = jnp.sum(state_one, axis=0)
    whole_total = jnp.sum(total_one, axis=0)
    fresh_state = jnp.sum(state_two, axis=0) / TOKENS
    fresh_total = jnp.sum(total_two, axis=0) / TOKENS
    shared_state = jnp.broadcast_to(whole_state, state_one.shape)
    shared_total = jnp.broadcast_to(whole_total, total_one.shape)
    moved_state = whole_state[None] - state_one + state_two
    moved_total = whole_total[None] - total_one + total_two
    grid_one = values[0].reshape(N_TM, ROWS_DEV, COLS, channels)
    grid_two = values[1].reshape(N_TM, ROWS_DEV, COLS, channels)
    upper_rim, lower_rim = rim_rows(grid_one)
    mixed_one = (spread(queries[0], shared_state, shared_total) + convolve(grid_one, upper_rim, lower_rim, conv_weight)).astype(jnp.bfloat16)
    mixed_two = (spread(queries[1], moved_state, moved_total) + convolve(grid_two, upper_rim, lower_rim, conv_weight)).astype(jnp.bfloat16)
    update_one = gates[0] * jnp.dot(mixed_one, out_weight, preferred_element_type=jnp.float32)
    update_two = gates[1] * jnp.dot(mixed_two, out_weight, preferred_element_type=jnp.float32)
    return jnp.stack([update_one, update_two]), fresh_state, fresh_total
```

```python
import functools

import jax
import jax.numpy as jnp
from jax import lax
from jax.experimental import pallas as pl
from jax.experimental.pallas import tpu as pltpu
from jax.sharding import PartitionSpec as P

NH = 16
HD = 70
COLS = 64
CH = NH * HD
LT = 128
NC = -(-CH // LT)
NR = 9
MESH = pl.DeviceIdType.MESH
F32 = jnp.float32
BF16 = jnp.bfloat16


def spans(width):
    out = []
    for c0 in range(0, CH, width):
        c1 = min(c0 + width, CH)
        h0, h1 = c0 // HD, (c1 - 1) // HD
        r0 = h0 * HD // LT * LT
        r1 = min(-(-(h1 + 1) * HD // LT) * LT, CH)
        out.append((c0, c1, h0, h1, r0, r1))
    return out


def local_state(k_ref, v_ref, s, part, band, put):
    tokens = k_ref.shape[1]
    ones = jnp.ones((8, tokens), BF16)
    for c, (c0, c1, h0, h1, r0, r1) in enumerate(spans(LT)):
        w = c1 - c0
        band[0 : r1 - r0, 0:w] = lax.dot_general(
            k_ref[s, :, r0:r1], v_ref[s, :, c0:c1], (((0,), (0,)), ((), ())), preferred_element_type=F32
        )
        count = jnp.dot(ones, k_ref[s, :, c0:c1], preferred_element_type=F32)[0:1]
        lane = c0 + lax.broadcasted_iota(jnp.int32, (NR * 8, w), 1)
        row = lax.broadcasted_iota(jnp.int32, (NR * 8, w), 0)
        tile = jnp.zeros((NR * 8, w), F32)
        for h in range(h0, h1 + 1):
            rows = band[h * HD - r0 : h * HD - r0 + NR * 8, 0:w]
            tile = jnp.where((lane >= h * HD) & (lane < (h + 1) * HD), rows, tile)
        tile = jnp.where(row < HD, tile, jnp.where(row == HD, count, 0.0))
        for r in range(NR):
            put(part, s, r * NC + c, w, tile[8 * r : 8 * r + 8])


def convolve(v_ref, s, rim, cw_ref, out_ref):
    tokens = v_ref.shape[1]
    for c0, c1, *_ in spans(LT):
        w = c1 - c0
        mid = v_ref[s, :, c0:c1].astype(F32)
        pad = jnp.concatenate([rim[0, :, c0:c1].astype(F32), mid, rim[1, :, c0:c1].astype(F32)], axis=0)
        col = lax.broadcasted_iota(jnp.int32, (tokens, w), 0) % COLS
        acc = None
        for b in range(3):
            one = sum(
                pad[a * COLS : a * COLS + tokens] * cw_ref[3 * a + b : 3 * a + b + 1, c0:c1] for a in range(3)
            )
            if b == 0:
                one = jnp.where(col != 0, pltpu.roll(one, 1, 0), 0.0)
            if b == 2:
                one = jnp.where(col != COLS - 1, pltpu.roll(one, tokens - 1, 0), 0.0)
            acc = one if acc is None else acc + one
        out_ref[s, :, c0:c1] = acc


def gather_kernel(
    n, m, k_ref, v_ref, cw_ref, st_ref, conv_ref,
    part, cin, cur, rin, full, rim, band,
    core_s, core_r, p1_s, p1_r, p2_s, p2_r, fw_s, fw_r, rim_s, rim_r,
):
    me = lax.axis_index("tm")
    half = n // 2
    core = me % 2
    chip = me // 2
    mate = chip * 2 + (1 - core)
    tokens = k_ref.shape[1]

    def at(k):
        return lax.rem(chip + k, half) * 2 + core

    def place(idx):
        g, j = idx // m, idx % m
        return g // half, g % half, j

    def put(ref, s, idx, w, value):
        c, p, j = place(idx)
        ref[s, c, p, j, :, 0:w] = value

    barrier = pltpu.get_barrier_semaphore()
    pl.semaphore_signal(barrier, inc=1, device_id={"tm": mate}, device_id_type=MESH)
    for k in range(1, half):
        pl.semaphore_signal(barrier, inc=1, device_id={"tm": at(k)}, device_id_type=MESH)
    beside = lax.rem(me + 2 * core - 1 + n, n)
    pl.semaphore_signal(barrier, inc=1, device_id={"tm": beside}, device_id_type=MESH)
    pl.semaphore_wait(barrier, half + 1)

    def remote(src, dst, ss, rs, dev):
        return pltpu.make_async_remote_copy(
            src_ref=src, dst_ref=dst, send_sem=ss, recv_sem=rs, device_id={"tm": dev}, device_id_type=MESH
        )

    def swap(s):
        return remote(part.at[s, 1 - core], cin.at[s], core_s.at[s], core_r.at[s], mate)

    def first(s, k):
        return remote(cur.at[s, lax.rem(chip + k, half)], rin.at[s, k], p1_s.at[s, k], p1_r.at[s, k], at(k))

    def second(s, k):
        return remote(
            full.at[s, core, chip], full.at[s, core, chip], p2_s.at[s, k], p2_r.at[s, k], at(k)
        )

    def second_in(s, k):
        src = lax.rem(chip + half - k, half)
        return remote(full.at[s, core, src], full.at[s, core, src], p2_s.at[s, k], p2_r.at[s, k], at(k))

    def onward(s, k):
        src = lax.rem(chip + half - k, half)
        return remote(full.at[s, core, src], full.at[s, core, src], fw_s.at[s, k], fw_r.at[s, k], mate)

    def onward_in(s, k):
        src = lax.rem(chip + half - k, half)
        return remote(full.at[s, 1 - core, src], full.at[s, 1 - core, src], fw_s.at[s, k], fw_r.at[s, k], mate)

    down = remote(v_ref.at[0, pl.ds(tokens - COLS, COLS)], rim.at[0], rim_s.at[0], rim_r.at[0], me + 1)
    up = remote(v_ref.at[0, pl.ds(0, COLS)], rim.at[1], rim_s.at[1], rim_r.at[1], me - 1)

    part[...] = jnp.zeros_like(part)
    local_state(k_ref, v_ref, 0, part, band, put)
    swap(0).start()

    @pl.when(me < n - 1)
    def _():
        down.start()

    @pl.when(me > 0)
    def _():
        up.start()

    local_state(k_ref, v_ref, 1, part, band, put)
    swap(1).start()
    for s in range(2):
        swap(s).wait()
        cur[s] = part[s, core] + cin[s]
        for k in range(1, half):
            first(s, k).start()

    @pl.when(me == 0)
    def _():
        rim[0] = jnp.zeros_like(rim[0])

    @pl.when(me == n - 1)
    def _():
        rim[1] = jnp.zeros_like(rim[1])

    @pl.when(me < n - 1)
    def _():
        down.wait_send()
        up.wait_recv()

    @pl.when(me > 0)
    def _():
        up.wait_send()
        down.wait_recv()

    for s in range(2):
        convolve(v_ref, s, rim, cw_ref, conv_ref)
        total = cur[s, chip]
        for k in range(1, half):
            first(s, k).wait()
            total = total + rin[s, k]
        full[s, core, chip] = total
        for k in range(1, half):
            second(s, k).start()
        onward(s, 0).start()
    for s in range(2):
        for k in range(1, half):
            second_in(s, k).wait_recv()
            onward(s, k).start()
        for k in range(1, half):
            second(s, k).wait_send()
    for s in range(2):
        for k in range(half):
            onward(s, k).wait_send()
            onward_in(s, k).wait_recv()
    for r in range(NR):
        for c in range(NC):
            where = place(r * NC + c)
            rows, cols = slice(8 * r, 8 * r + 8), slice(LT * c, LT * c + LT)
            whole = full[(0, *where)]
            st_ref[0, rows, cols] = whole
            st_ref[1, rows, cols] = whole - part[(0, *where)] + part[(1, *where)]
            st_ref[2, rows, cols] = full[(1, *where)]


def split(x):
    high = x.astype(BF16)
    return high, (x - high.astype(F32)).astype(BF16)


def mix(q_ref, st_ref, conv_ref, s, mixed, block):
    tokens = q_ref.shape[1]
    for c0, c1, h0, h1, r0, r1 in spans(256):
        w, depth = c1 - c0, r1 - r0
        block[...] = jnp.zeros_like(block)
        state = st_ref[s, 0:72, c0:c1]
        lane = c0 + lax.broadcasted_iota(jnp.int32, (HD, w), 1)
        for h in range(h0, h1 + 1):
            block[h * HD - r0 : (h + 1) * HD - r0, 0:w] = jnp.where(
                (lane >= h * HD) & (lane < (h + 1) * HD), state[0:HD], 0.0
            )
        high, low = split(block[0:depth, 0:w])
        query = q_ref[s, :, r0:r1]
        numer = jnp.dot(query, high, preferred_element_type=F32) + jnp.dot(
            query, low, preferred_element_type=F32
        )
        row_head = jnp.floor((lax.broadcasted_iota(jnp.int32, (depth, w), 0).astype(F32) + (r0 + 0.5)) / HD)
        col_head = jnp.floor((lax.broadcasted_iota(jnp.int32, (depth, w), 1).astype(F32) + (c0 + 0.5)) / HD)
        same = (row_head == col_head).astype(F32).astype(BF16)
        high, low = split(query.astype(F32) * st_ref[s, HD : HD + 1, r0:r1])
        denom = jnp.dot(high, same, preferred_element_type=F32) + jnp.dot(low, same, preferred_element_type=F32)
        mixed[s * tokens : (s + 1) * tokens, c0:c1] = (numer / denom + conv_ref[s, :, c0:c1]).astype(BF16)


def project_kernel(
    total_tokens, ts_ref, q_ref, st_ref, conv_ref, gate_ref, w_ref, out_ref, fs_ref, ft_ref, mixed, block
):
    tokens = q_ref.shape[1]

    @pl.when(pl.program_id(0) == 0)
    def _():
        for s in range(2):
            mix(q_ref, st_ref, conv_ref, s, mixed, block)
        for h in range(NH):
            base = min(h * HD // LT * LT, NC * LT - 2 * LT)
            both = st_ref[2, :, base : base + 2 * LT] / total_tokens
            both = pltpu.roll(both, (2 * LT - (h * HD - base)) % (2 * LT), 1)
            fs_ref[h] = both[0:HD, 0:HD]
            ft_ref[h : h + 1, :] = both[HD : HD + 1, 0:HD]

    for s in range(2):
        acc = jnp.dot(mixed[s * tokens : (s + 1) * tokens, :], w_ref[...], preferred_element_type=F32)
        out_ref[s] = gate_ref[pl.ds(ts_ref[s], 1), :] * acc


def local(n, queries, keys, values, timesteps, gate_table, out_weight, conv_weight):
    tokens = queries.shape[1]
    width = out_weight.shape[1]
    half = n // 2
    m = -(-NR * NC // n)
    vmem = pl.BlockSpec(memory_space=pltpu.VMEM)
    dma = pltpu.SemaphoreType.DMA
    states, conv = pl.pallas_call(
        functools.partial(gather_kernel, n, m),
        out_shape=(
            jax.ShapeDtypeStruct((3, NR * 8, NC * LT), F32),
            jax.ShapeDtypeStruct((2, tokens, CH), F32),
        ),
        in_specs=[vmem] * 3,
        out_specs=(vmem, vmem),
        scratch_shapes=[
            pltpu.VMEM((2, 2, half, m, 8, LT), F32),
            pltpu.VMEM((2, half, m, 8, LT), F32),
            pltpu.VMEM((2, half, m, 8, LT), F32),
            pltpu.VMEM((2, half, m, 8, LT), F32),
            pltpu.VMEM((2, 2, half, m, 8, LT), F32),
            pltpu.VMEM((2, COLS, CH), BF16),
            pltpu.VMEM((640, LT), F32),
            dma((2,)), dma((2,)),
            dma((2, half)), dma((2, half)),
            dma((2, half)), dma((2, half)),
            dma((2, half)), dma((2, half)),
            dma((2,)), dma((2,)),
        ],
        compiler_params=pltpu.CompilerParams(
            collective_id=0, has_side_effects=True, vmem_limit_bytes=40 * 2**20
        ),
        name="states",
    )(keys, values, conv_weight)
    nb = 640
    once = lambda shape: pl.BlockSpec(shape, lambda i, ts: (0,) * len(shape), pipeline_mode=pl.Buffered(1))
    return pl.pallas_call(
        functools.partial(project_kernel, float(tokens * n)),
        out_shape=(
            jax.ShapeDtypeStruct((2, tokens, width), F32),
            jax.ShapeDtypeStruct((NH, HD, HD), F32),
            jax.ShapeDtypeStruct((NH, HD), F32),
        ),
        grid_spec=pltpu.PrefetchScalarGridSpec(
            num_scalar_prefetch=1,
            grid=(pl.cdiv(width, nb),),
            in_specs=[
                once((2, tokens, CH)),
                once((3, NR * 8, NC * LT)),
                once((2, tokens, CH)),
                pl.BlockSpec((gate_table.shape[0], nb), lambda i, ts: (0, i)),
                pl.BlockSpec((CH, nb), lambda i, ts: (0, i)),
            ],
            out_specs=(
                pl.BlockSpec((2, tokens, nb), lambda i, ts: (0, 0, i)),
                pl.BlockSpec((NH, HD, HD), lambda i, ts: (0, 0, 0)),
                pl.BlockSpec((NH, HD), lambda i, ts: (0, 0)),
            ),
            scratch_shapes=[pltpu.VMEM((2 * tokens, CH), BF16), pltpu.VMEM((640, 256), F32)],
        ),
        compiler_params=pltpu.CompilerParams(
            dimension_semantics=("arbitrary",), vmem_limit_bytes=40 * 2**20
        ),
        name="project",
    )(timesteps, queries, states, conv, gate_table, out_weight)


def solution(mesh):
    n = mesh.shape["tm"]
    placed = (
        P(None, ("grp", "tm"), None),
        P(None, ("grp", "tm"), None),
        P(None, ("grp", "tm"), None),
        P("grp"),
        P(),
        P(),
        P(),
    )
    return jax.shard_map(
        functools.partial(local, n),
        mesh=mesh,
        in_specs=placed,
        out_specs=(P(None, ("grp", "tm"), None), P("grp", None, None), P("grp", None)),
        check_vma=False,
    )
```

```python
import functools

import jax
import jax.numpy as jnp
from jax import lax
from jax.experimental import pallas as pl
from jax.experimental.pallas import tpu as pltpu
from jax.sharding import PartitionSpec as P

NH = 16
HD = 70
COLS = 64
CH = NH * HD
LT = 128
NC = -(-CH // LT)
NR = 9
MESH = pl.DeviceIdType.MESH
F32 = jnp.float32
BF16 = jnp.bfloat16


def spans(width):
    out = []
    for c0 in range(0, CH, width):
        c1 = min(c0 + width, CH)
        h0, h1 = c0 // HD, (c1 - 1) // HD
        r0 = h0 * HD // LT * LT
        r1 = min(-(-(h1 + 1) * HD // LT) * LT, CH)
        out.append((c0, c1, h0, h1, r0, r1))
    return out


def local_state(k_ref, v_ref, s, part, band, put):
    ones = jnp.ones((8, k_ref.shape[2]), BF16)
    lanes = (((1,), (1,)), ((), ()))
    for c, (c0, c1, h0, h1, r0, r1) in enumerate(spans(LT)):
        w = c1 - c0
        band[0 : r1 - r0, 0:w] = lax.dot_general(
            k_ref[s, r0:r1, :], v_ref[s, c0:c1, :], lanes, preferred_element_type=F32
        )
        count = lax.dot_general(ones, k_ref[s, c0:c1, :], lanes, preferred_element_type=F32)[0:1]
        lane = c0 + lax.broadcasted_iota(jnp.int32, (NR * 8, w), 1)
        row = lax.broadcasted_iota(jnp.int32, (NR * 8, w), 0)
        tile = jnp.zeros((NR * 8, w), F32)
        for h in range(h0, h1 + 1):
            rows = band[h * HD - r0 : h * HD - r0 + NR * 8, 0:w]
            tile = jnp.where((lane >= h * HD) & (lane < (h + 1) * HD), rows, tile)
        tile = jnp.where(row < HD, tile, jnp.where(row == HD, count, 0.0))
        for r in range(NR):
            put(part, s, r * NC + c, w, tile[8 * r : 8 * r + 8])


def pack(v_ref, lower, out_ref):
    base = v_ref.shape[2] - LT if lower else 0
    lane = lax.broadcasted_iota(jnp.int32, (CH // 2, LT), 1)
    one = v_ref[0, 0 : CH // 2, base : base + LT].astype(F32)
    two = pltpu.roll(v_ref[0, CH // 2 : CH, base : base + LT].astype(F32), LT // 2, 1)
    keep = lane >= LT // 2 if lower else lane < LT // 2
    out_ref[...] = jnp.where(keep, one, two).astype(BF16)


def unpack(rim_ref, rims):
    lane_block = rim_ref[...].astype(F32)
    rims[0 : CH // 2] = pltpu.roll(lane_block, LT // 2, 1)
    rims[CH // 2 : CH] = lane_block


def convolve(v_ref, s, above, below, taps, out_ref):
    tokens = v_ref.shape[2]
    step = CH // 10
    lane = lax.broadcasted_iota(jnp.int32, (step, tokens), 1)
    col = lane % COLS
    for c0 in range(0, CH, step):
        mid = v_ref[s, c0 : c0 + step, :].astype(F32)
        top = above[c0 : c0 + step, :]
        low = below[c0 : c0 + step, :]
        blank = jnp.zeros((step, tokens - LT), F32)
        rows = (
            jnp.where(lane < COLS, jnp.concatenate([top, blank], axis=1), pltpu.roll(mid, COLS, 1)),
            mid,
            jnp.where(
                lane >= tokens - COLS, jnp.concatenate([blank, low], axis=1), pltpu.roll(mid, tokens - COLS, 1)
            ),
        )
        acc = None
        for b in range(3):
            one = sum(rows[a] * taps[c0 : c0 + step, 3 * a + b : 3 * a + b + 1] for a in range(3))
            if b == 0:
                one = jnp.where(col != 0, pltpu.roll(one, 1, 1), 0.0)
            if b == 2:
                one = jnp.where(col != COLS - 1, pltpu.roll(one, tokens - 1, 1), 0.0)
            acc = one if acc is None else acc + one
        out_ref[s, c0 : c0 + step, :] = acc


def gather_kernel(
    n, m, k_ref, v_ref, cw_ref, st_ref, conv_ref,
    part, cin, cur, rin, full, edge, rim, above, below, wide, taps, band,
    core_s, core_r, p1_s, p1_r, p2_s, p2_r, fw_s, fw_r, rim_s, rim_r,
):
    me = lax.axis_index("tm")
    half = n // 2
    core = me % 2
    chip = me // 2
    mate = chip * 2 + (1 - core)

    def at(k):
        return lax.rem(chip + k, half) * 2 + core

    def place(idx):
        g, j = idx // m, idx % m
        return g // half, g % half, j

    def put(ref, s, idx, w, value):
        c, p, j = place(idx)
        ref[s, c, p, j, :, 0:w] = value

    barrier = pltpu.get_barrier_semaphore()
    pl.semaphore_signal(barrier, inc=1, device_id={"tm": mate}, device_id_type=MESH)
    for k in range(1, half):
        pl.semaphore_signal(barrier, inc=1, device_id={"tm": at(k)}, device_id_type=MESH)
    beside = lax.rem(me + 2 * core - 1 + n, n)
    pl.semaphore_signal(barrier, inc=1, device_id={"tm": beside}, device_id_type=MESH)
    pl.semaphore_wait(barrier, half + 1)

    def remote(src, dst, ss, rs, dev):
        return pltpu.make_async_remote_copy(
            src_ref=src, dst_ref=dst, send_sem=ss, recv_sem=rs, device_id={"tm": dev}, device_id_type=MESH
        )

    def swap(s):
        return remote(part.at[s, 1 - core], cin.at[s], core_s.at[s], core_r.at[s], mate)

    def first(s, k):
        return remote(cur.at[s, lax.rem(chip + k, half)], rin.at[s, k], p1_s.at[s, k], p1_r.at[s, k], at(k))

    def second(s, k):
        return remote(
            full.at[s, core, chip], full.at[s, core, chip], p2_s.at[s, k], p2_r.at[s, k], at(k)
        )

    def second_in(s, k):
        src = lax.rem(chip + half - k, half)
        return remote(full.at[s, core, src], full.at[s, core, src], p2_s.at[s, k], p2_r.at[s, k], at(k))

    def onward(s, k):
        src = lax.rem(chip + half - k, half)
        return remote(full.at[s, core, src], full.at[s, core, src], fw_s.at[s, k], fw_r.at[s, k], mate)

    def onward_in(s, k):
        src = lax.rem(chip + half - k, half)
        return remote(full.at[s, 1 - core, src], full.at[s, 1 - core, src], fw_s.at[s, k], fw_r.at[s, k], mate)

    down = remote(edge.at[0], rim.at[0], rim_s.at[0], rim_r.at[0], me + 1)
    up = remote(edge.at[1], rim.at[1], rim_s.at[1], rim_r.at[1], me - 1)

    part[...] = jnp.zeros_like(part)
    local_state(k_ref, v_ref, 0, part, band, put)
    swap(0).start()
    pack(v_ref, True, edge.at[0])
    pack(v_ref, False, edge.at[1])

    @pl.when(me < n - 1)
    def _():
        down.start()

    @pl.when(me > 0)
    def _():
        up.start()

    local_state(k_ref, v_ref, 1, part, band, put)
    swap(1).start()
    wide[...] = jnp.zeros_like(wide)
    wide[0:9, 0:CH] = cw_ref[...]
    for c in range(NC):
        taps[LT * c : LT * c + LT, :] = jnp.transpose(wide[:, LT * c : LT * c + LT])
    for s in range(2):
        swap(s).wait()
        cur[s] = part[s, core] + cin[s]
        for k in range(1, half):
            first(s, k).start()

    @pl.when(me == 0)
    def _():
        rim[0] = jnp.zeros_like(rim[0])

    @pl.when(me == n - 1)
    def _():
        rim[1] = jnp.zeros_like(rim[1])

    @pl.when(me < n - 1)
    def _():
        down.wait_send()
        up.wait_recv()

    @pl.when(me > 0)
    def _():
        up.wait_send()
        down.wait_recv()

    unpack(rim.at[0], above)
    unpack(rim.at[1], below)
    for s in range(2):
        convolve(v_ref, s, above, below, taps, conv_ref)
        total = cur[s, chip]
        for k in range(1, half):
            first(s, k).wait()
            total = total + rin[s, k]
        full[s, core, chip] = total
        for k in range(1, half):
            second(s, k).start()
        onward(s, 0).start()
    for s in range(2):
        for k in range(1, half):
            second_in(s, k).wait_recv()
            onward(s, k).start()
        for k in range(1, half):
            second(s, k).wait_send()
    for s in range(2):
        for k in range(half):
            onward(s, k).wait_send()
            onward_in(s, k).wait_recv()
    for r in range(NR):
        for c in range(NC):
            where = place(r * NC + c)
            rows, cols = slice(8 * r, 8 * r + 8), slice(LT * c, LT * c + LT)
            whole = full[(0, *where)]
            st_ref[0, rows, cols] = whole
            st_ref[1, rows, cols] = whole - part[(0, *where)] + part[(1, *where)]
            st_ref[2, rows, cols] = full[(1, *where)]


def split(x):
    high = x.astype(BF16)
    return high, (x - high.astype(F32)).astype(BF16)


def mix(q_ref, st_ref, conv_ref, s, mixed, block):
    tokens = q_ref.shape[2]
    firsts = (((0,), (0,)), ((), ()))
    for c0, c1, h0, h1, r0, r1 in spans(256):
        w, depth = c1 - c0, r1 - r0
        block[...] = jnp.zeros_like(block)
        state = st_ref[s, 0:72, c0:c1]
        lane = c0 + lax.broadcasted_iota(jnp.int32, (HD, w), 1)
        for h in range(h0, h1 + 1):
            block[h * HD - r0 : (h + 1) * HD - r0, 0:w] = jnp.where(
                (lane >= h * HD) & (lane < (h + 1) * HD), state[0:HD], 0.0
            )
        query = q_ref[s, r0:r1, :]
        numer = sum(
            lax.dot_general(x, query, firsts, preferred_element_type=F32) for x in split(block[0:depth, 0:w])
        )
        row_head = jnp.floor((lax.broadcasted_iota(jnp.int32, (w, depth), 0).astype(F32) + (c0 + 0.5)) / HD)
        col_head = jnp.floor((lax.broadcasted_iota(jnp.int32, (w, depth), 1).astype(F32) + (r0 + 0.5)) / HD)
        norm = jnp.where(row_head == col_head, st_ref[s, HD : HD + 1, r0:r1], 0.0)
        denom = sum(jnp.dot(x, query, preferred_element_type=F32) for x in split(norm))
        mixed[c0:c1, s * tokens : (s + 1) * tokens] = (numer / denom + conv_ref[s, c0:c1, :]).astype(BF16)


def project_kernel(
    total_tokens, ts_ref, q_ref, st_ref, conv_ref, gate_ref, w_ref, out_ref, fs_ref, ft_ref, mixed, block, gates
):
    tokens = q_ref.shape[2]

    @pl.when(pl.program_id(0) == 0)
    def _():
        for s in range(2):
            mix(q_ref, st_ref, conv_ref, s, mixed, block)
        for h in range(NH):
            base = min(h * HD // LT * LT, NC * LT - 2 * LT)
            both = st_ref[2, :, base : base + 2 * LT] / total_tokens
            both = pltpu.roll(both, (2 * LT - (h * HD - base)) % (2 * LT), 1)
            fs_ref[h] = both[0:HD, 0:HD]
            ft_ref[h : h + 1, :] = both[HD : HD + 1, 0:HD]

    for s in range(2):
        gates[s : s + 1, :] = gate_ref[pl.ds(ts_ref[s], 1), :]
    acc = lax.dot_general(w_ref[...], mixed[...], (((0,), (0,)), ((), ())), preferred_element_type=F32)
    for c in range(0, acc.shape[0], LT):
        gate = jnp.transpose(gates[:, c : c + LT])
        for s in range(2):
            out_ref[s, c : c + LT, :] = gate[:, s : s + 1] * acc[c : c + LT, s * tokens : (s + 1) * tokens]


def local(n, queries, keys, values, timesteps, gate_table, out_weight, conv_weight):
    tokens = queries.shape[1]
    width = out_weight.shape[1]
    half = n // 2
    queries, keys, values = (jnp.swapaxes(x, 1, 2) for x in (queries, keys, values))
    m = -(-NR * NC // n)
    vmem = pl.BlockSpec(memory_space=pltpu.VMEM)
    dma = pltpu.SemaphoreType.DMA
    states, conv = pl.pallas_call(
        functools.partial(gather_kernel, n, m),
        out_shape=(
            jax.ShapeDtypeStruct((3, NR * 8, NC * LT), F32),
            jax.ShapeDtypeStruct((2, CH, tokens), F32),
        ),
        in_specs=[vmem] * 3,
        out_specs=(vmem, vmem),
        scratch_shapes=[
            pltpu.VMEM((2, 2, half, m, 8, LT), F32),
            pltpu.VMEM((2, half, m, 8, LT), F32),
            pltpu.VMEM((2, half, m, 8, LT), F32),
            pltpu.VMEM((2, half, m, 8, LT), F32),
            pltpu.VMEM((2, 2, half, m, 8, LT), F32),
            pltpu.VMEM((2, CH // 2, LT), BF16),
            pltpu.VMEM((2, CH // 2, LT), BF16),
            pltpu.VMEM((CH, LT), F32),
            pltpu.VMEM((CH, LT), F32),
            pltpu.VMEM((LT, NC * LT), F32),
            pltpu.VMEM((NC * LT, LT), F32),
            pltpu.VMEM((640, LT), F32),
            dma((2,)), dma((2,)),
            dma((2, half)), dma((2, half)),
            dma((2, half)), dma((2, half)),
            dma((2, half)), dma((2, half)),
            dma((2,)), dma((2,)),
        ],
        compiler_params=pltpu.CompilerParams(
            collective_id=0, has_side_effects=True, vmem_limit_bytes=20 * 2**20
        ),
        name="states",
    )(keys, values, conv_weight)
    nb = 640
    once = lambda shape: pl.BlockSpec(shape, lambda i, ts: (0,) * len(shape), pipeline_mode=pl.Buffered(1))
    update, fresh, total = pl.pallas_call(
        functools.partial(project_kernel, float(tokens * n)),
        out_shape=(
            jax.ShapeDtypeStruct((2, width, tokens), F32),
            jax.ShapeDtypeStruct((NH, HD, HD), F32),
            jax.ShapeDtypeStruct((NH, HD), F32),
        ),
        grid_spec=pltpu.PrefetchScalarGridSpec(
            num_scalar_prefetch=1,
            grid=(pl.cdiv(width, nb),),
            in_specs=[
                once((2, CH, tokens)),
                once((3, NR * 8, NC * LT)),
                once((2, CH, tokens)),
                pl.BlockSpec((gate_table.shape[0], nb), lambda i, ts: (0, i)),
                pl.BlockSpec((CH, nb), lambda i, ts: (0, i)),
            ],
            out_specs=(
                pl.BlockSpec((2, nb, tokens), lambda i, ts: (0, i, 0)),
                pl.BlockSpec((NH, HD, HD), lambda i, ts: (0, 0, 0)),
                pl.BlockSpec((NH, HD), lambda i, ts: (0, 0)),
            ),
            scratch_shapes=[
                pltpu.VMEM((CH, 2 * tokens), BF16),
                pltpu.VMEM((640, 256), F32),
                pltpu.VMEM((LT, nb), F32),
            ],
        ),
        compiler_params=pltpu.CompilerParams(
            dimension_semantics=("arbitrary",), vmem_limit_bytes=28 * 2**20
        ),
        name="project",
    )(timesteps, queries, states, conv, gate_table, out_weight)
    return jnp.swapaxes(update, 1, 2), fresh, total


def solution(mesh):
    n = mesh.shape["tm"]
    placed = (
        P(None, ("grp", "tm"), None),
        P(None, ("grp", "tm"), None),
        P(None, ("grp", "tm"), None),
        P("grp"),
        P(),
        P(),
        P(),
    )
    return jax.shard_map(
        functools.partial(local, n),
        mesh=mesh,
        in_specs=placed,
        out_specs=(P(None, ("grp", "tm"), None), P("grp", None, None), P("grp", None)),
        check_vma=False,
    )
```

```python
import functools

import jax
import jax.numpy as jnp
from jax import lax
from jax.experimental import pallas as pl
from jax.experimental.pallas import tpu as pltpu
from jax.sharding import PartitionSpec as P

NH = 16
HD = 70
COLS = 64
CH = NH * HD
LT = 128
NC = -(-CH // LT)
NR = 9
TILES = NR * NC - 1
SPARE = NC * LT - CH
EDGE = LT - SPARE
MESH = pl.DeviceIdType.MESH
F32 = jnp.float32
BF16 = jnp.bfloat16


def spans(width):
    out = []
    for c0 in range(0, CH, width):
        c1 = min(c0 + width, CH)
        h0, h1 = c0 // HD, (c1 - 1) // HD
        r0 = h0 * HD // LT * LT
        r1 = min(-(-(h1 + 1) * HD // LT) * LT, CH)
        out.append((c0, c1, h0, h1, r0, r1))
    return out


def local_state(k_ref, v_ref, s, part, band, put):
    ones = jnp.ones((8, k_ref.shape[2]), BF16)
    lanes = (((1,), (1,)), ((), ()))
    for c, (c0, c1, h0, h1, r0, r1) in enumerate(spans(LT)):
        w = c1 - c0
        band[0 : r1 - r0, 0:w] = lax.dot_general(
            k_ref[s, r0:r1, :], v_ref[s, c0:c1, :], lanes, preferred_element_type=F32
        )
        count = lax.dot_general(ones, k_ref[s, c0:c1, :], lanes, preferred_element_type=F32)[0:1]
        lane = c0 + lax.broadcasted_iota(jnp.int32, (NR * 8, w), 1)
        row = lax.broadcasted_iota(jnp.int32, (NR * 8, w), 0)
        tile = jnp.zeros((NR * 8, w), F32)
        for h in range(h0, h1 + 1):
            rows = band[h * HD - r0 : h * HD - r0 + NR * 8, 0:w]
            tile = jnp.where((lane >= h * HD) & (lane < (h + 1) * HD), rows, tile)
        tile = jnp.where(row < HD, tile, jnp.where(row == HD, count, 0.0))
        for r in range(NR - (c == NC - 1)):
            put(part, s, r * NC + c, slice(0, w), tile[8 * r : 8 * r + 8])
        if c == NC - 1:
            for i in range(EDGE // SPARE):
                piece = tile[8 * NR - 8 :, SPARE * i : SPARE * i + SPARE]
                put(part, s, i * NC + c, slice(EDGE, LT), piece)


def pack(v_ref, lower, out_ref):
    base = v_ref.shape[2] - LT if lower else 0
    lane = lax.broadcasted_iota(jnp.int32, (CH // 2, LT), 1)
    one = v_ref[0, 0 : CH // 2, base : base + LT].astype(F32)
    two = pltpu.roll(v_ref[0, CH // 2 : CH, base : base + LT].astype(F32), LT // 2, 1)
    keep = lane >= LT // 2 if lower else lane < LT // 2
    out_ref[...] = jnp.where(keep, one, two).astype(BF16)


def unpack(rim_ref, rims):
    lane_block = rim_ref[...].astype(F32)
    rims[0 : CH // 2] = pltpu.roll(lane_block, LT // 2, 1)
    rims[CH // 2 : CH] = lane_block


def convolve(v_ref, s, above, below, taps, out_ref):
    tokens = v_ref.shape[2]
    step = CH // 10
    lane = lax.broadcasted_iota(jnp.int32, (step, tokens), 1)
    col = lane % COLS
    for c0 in range(0, CH, step):
        mid = v_ref[s, c0 : c0 + step, :].astype(F32)
        top = above[c0 : c0 + step, :]
        low = below[c0 : c0 + step, :]
        blank = jnp.zeros((step, tokens - LT), F32)
        rows = (
            jnp.where(lane < COLS, jnp.concatenate([top, blank], axis=1), pltpu.roll(mid, COLS, 1)),
            mid,
            jnp.where(
                lane >= tokens - COLS, jnp.concatenate([blank, low], axis=1), pltpu.roll(mid, tokens - COLS, 1)
            ),
        )
        acc = None
        for b in range(3):
            one = sum(rows[a] * taps[c0 : c0 + step, 3 * a + b : 3 * a + b + 1] for a in range(3))
            if b == 0:
                one = jnp.where(col != 0, pltpu.roll(one, 1, 1), 0.0)
            if b == 2:
                one = jnp.where(col != COLS - 1, pltpu.roll(one, tokens - 1, 1), 0.0)
            acc = one if acc is None else acc + one
        out_ref[s, c0 : c0 + step, :] = acc


def gather_kernel(
    n, m, k_ref, v_ref, cw_ref, st_ref, conv_ref,
    part, cin, cur, rin, full, edge, rim, above, below, wide, taps, band,
    core_s, core_r, p1_s, p1_r, p2_s, p2_r, fw_s, fw_r, rim_s, rim_r,
):
    me = lax.axis_index("tm")
    half = n // 2
    core = me % 2
    chip = me // 2
    mate = chip * 2 + (1 - core)

    def at(k):
        return lax.rem(chip + k, half) * 2 + core

    def place(idx):
        g, j = idx // m, idx % m
        return g // half, g % half, j

    def put(ref, s, idx, lanes, value):
        c, p, j = place(idx)
        ref[s, c, p, j, :, lanes] = value

    barrier = pltpu.get_barrier_semaphore()
    pl.semaphore_signal(barrier, inc=1, device_id={"tm": mate}, device_id_type=MESH)
    for k in range(1, half):
        pl.semaphore_signal(barrier, inc=1, device_id={"tm": at(k)}, device_id_type=MESH)
    beside = lax.rem(me + 2 * core - 1 + n, n)
    pl.semaphore_signal(barrier, inc=1, device_id={"tm": beside}, device_id_type=MESH)
    pl.semaphore_wait(barrier, half + 1)

    def remote(src, dst, ss, rs, dev):
        return pltpu.make_async_remote_copy(
            src_ref=src, dst_ref=dst, send_sem=ss, recv_sem=rs, device_id={"tm": dev}, device_id_type=MESH
        )

    def swap(s):
        return remote(part.at[s, 1 - core], cin.at[s], core_s.at[s], core_r.at[s], mate)

    def first(s, k):
        return remote(cur.at[s, lax.rem(chip + k, half)], rin.at[s, k], p1_s.at[s, k], p1_r.at[s, k], at(k))

    def second(s, k):
        return remote(
            full.at[s, core, chip], full.at[s, core, chip], p2_s.at[s, k], p2_r.at[s, k], at(k)
        )

    def second_in(s, k):
        src = lax.rem(chip + half - k, half)
        return remote(full.at[s, core, src], full.at[s, core, src], p2_s.at[s, k], p2_r.at[s, k], at(k))

    def onward(s, k):
        src = lax.rem(chip + half - k, half)
        return remote(full.at[s, core, src], full.at[s, core, src], fw_s.at[s, k], fw_r.at[s, k], mate)

    def onward_in(s, k):
        src = lax.rem(chip + half - k, half)
        return remote(full.at[s, 1 - core, src], full.at[s, 1 - core, src], fw_s.at[s, k], fw_r.at[s, k], mate)

    down = remote(edge.at[0], rim.at[0], rim_s.at[0], rim_r.at[0], me + 1)
    up = remote(edge.at[1], rim.at[1], rim_s.at[1], rim_r.at[1], me - 1)

    part[...] = jnp.zeros_like(part)
    local_state(k_ref, v_ref, 0, part, band, put)
    swap(0).start()
    pack(v_ref, True, edge.at[0])
    pack(v_ref, False, edge.at[1])

    @pl.when(me < n - 1)
    def _():
        down.start()

    @pl.when(me > 0)
    def _():
        up.start()

    local_state(k_ref, v_ref, 1, part, band, put)
    swap(1).start()
    wide[...] = jnp.zeros_like(wide)
    wide[0:9, 0:CH] = cw_ref[...]
    for c in range(NC):
        taps[LT * c : LT * c + LT, :] = jnp.transpose(wide[:, LT * c : LT * c + LT])
    for s in range(2):
        swap(s).wait()
        cur[s] = part[s, core] + cin[s]
        for k in range(1, half):
            first(s, k).start()

    @pl.when(me == 0)
    def _():
        rim[0] = jnp.zeros_like(rim[0])

    @pl.when(me == n - 1)
    def _():
        rim[1] = jnp.zeros_like(rim[1])

    @pl.when(me < n - 1)
    def _():
        down.wait_send()
        up.wait_recv()

    @pl.when(me > 0)
    def _():
        up.wait_send()
        down.wait_recv()

    unpack(rim.at[0], above)
    unpack(rim.at[1], below)
    for s in range(2):
        convolve(v_ref, s, above, below, taps, conv_ref)
        total = cur[s, chip]
        for k in range(1, half):
            first(s, k).wait()
            total = total + rin[s, k]
        full[s, core, chip] = total
        for k in range(1, half):
            second(s, k).start()
        onward(s, 0).start()
    for s in range(2):
        for k in range(1, half):
            second_in(s, k).wait_recv()
            onward(s, k).start()
        for k in range(1, half):
            second(s, k).wait_send()
    for s in range(2):
        for k in range(half):
            onward(s, k).wait_send()
            onward_in(s, k).wait_recv()
    for idx in range(TILES):
        r, c = idx // NC, idx % NC
        where = place(idx)
        whole = full[(0, *where)]
        moved = whole - part[(0, *where)] + part[(1, *where)]
        for i, tile in enumerate((whole, moved, full[(1, *where)])):
            st_ref[i, 8 * r : 8 * r + 8, LT * c : LT * c + LT] = tile
            if c == NC - 1 and r < EDGE // SPARE:
                lane = LT * c + SPARE * r
                st_ref[i, 8 * NR - 8 :, lane : lane + SPARE] = tile[:, EDGE:]


def split(x):
    high = x.astype(BF16)
    return high, (x - high.astype(F32)).astype(BF16)


def mix(q_ref, st_ref, conv_ref, s, mixed, block):
    tokens = q_ref.shape[2]
    firsts = (((0,), (0,)), ((), ()))
    for c0, c1, h0, h1, r0, r1 in spans(256):
        w, depth = c1 - c0, r1 - r0
        block[...] = jnp.zeros_like(block)
        state = st_ref[s, 0:72, c0:c1]
        lane = c0 + lax.broadcasted_iota(jnp.int32, (HD, w), 1)
        for h in range(h0, h1 + 1):
            block[h * HD - r0 : (h + 1) * HD - r0, 0:w] = jnp.where(
                (lane >= h * HD) & (lane < (h + 1) * HD), state[0:HD], 0.0
            )
        query = q_ref[s, r0:r1, :]
        numer = sum(
            lax.dot_general(x, query, firsts, preferred_element_type=F32) for x in split(block[0:depth, 0:w])
        )
        row_head = jnp.floor((lax.broadcasted_iota(jnp.int32, (w, depth), 0).astype(F32) + (c0 + 0.5)) / HD)
        col_head = jnp.floor((lax.broadcasted_iota(jnp.int32, (w, depth), 1).astype(F32) + (r0 + 0.5)) / HD)
        norm = jnp.where(row_head == col_head, st_ref[s, HD : HD + 1, r0:r1], 0.0)
        denom = sum(jnp.dot(x, query, preferred_element_type=F32) for x in split(norm))
        mixed[c0:c1, s * tokens : (s + 1) * tokens] = (numer / denom + conv_ref[s, c0:c1, :]).astype(BF16)


def project_kernel(
    total_tokens, ts_ref, q_ref, st_ref, conv_ref, gate_ref, w_ref, out_ref, fs_ref, ft_ref, mixed, block, gates
):
    tokens = q_ref.shape[2]

    @pl.when(pl.program_id(0) == 0)
    def _():
        for s in range(2):
            mix(q_ref, st_ref, conv_ref, s, mixed, block)
        for h in range(NH):
            base = min(h * HD // LT * LT, NC * LT - 2 * LT)
            both = st_ref[2, :, base : base + 2 * LT] / total_tokens
            both = pltpu.roll(both, (2 * LT - (h * HD - base)) % (2 * LT), 1)
            fs_ref[h] = both[0:HD, 0:HD]
            ft_ref[h : h + 1, :] = both[HD : HD + 1, 0:HD]

    for s in range(2):
        gates[s : s + 1, :] = gate_ref[pl.ds(ts_ref[s], 1), :]
    acc = lax.dot_general(w_ref[...], mixed[...], (((0,), (0,)), ((), ())), preferred_element_type=F32)
    for c in range(0, acc.shape[0], LT):
        gate = jnp.transpose(gates[:, c : c + LT])
        for s in range(2):
            out_ref[s, c : c + LT, :] = gate[:, s : s + 1] * acc[c : c + LT, s * tokens : (s + 1) * tokens]


def local(n, queries, keys, values, timesteps, gate_table, out_weight, conv_weight):
    tokens = queries.shape[1]
    width = out_weight.shape[1]
    half = n // 2
    queries, keys, values = (jnp.swapaxes(x, 1, 2) for x in (queries, keys, values))
    m = -(-TILES // n)
    vmem = pl.BlockSpec(memory_space=pltpu.VMEM)
    dma = pltpu.SemaphoreType.DMA
    states, conv = pl.pallas_call(
        functools.partial(gather_kernel, n, m),
        out_shape=(
            jax.ShapeDtypeStruct((3, NR * 8, NC * LT), F32),
            jax.ShapeDtypeStruct((2, CH, tokens), F32),
        ),
        in_specs=[vmem] * 3,
        out_specs=(vmem, vmem),
        scratch_shapes=[
            pltpu.VMEM((2, 2, half, m, 8, LT), F32),
            pltpu.VMEM((2, half, m, 8, LT), F32),
            pltpu.VMEM((2, half, m, 8, LT), F32),
            pltpu.VMEM((2, half, m, 8, LT), F32),
            pltpu.VMEM((2, 2, half, m, 8, LT), F32),
            pltpu.VMEM((2, CH // 2, LT), BF16),
            pltpu.VMEM((2, CH // 2, LT), BF16),
            pltpu.VMEM((CH, LT), F32),
            pltpu.VMEM((CH, LT), F32),
            pltpu.VMEM((LT, NC * LT), F32),
            pltpu.VMEM((NC * LT, LT), F32),
            pltpu.VMEM((640, LT), F32),
            dma((2,)), dma((2,)),
            dma((2, half)), dma((2, half)),
            dma((2, half)), dma((2, half)),
            dma((2, half)), dma((2, half)),
            dma((2,)), dma((2,)),
        ],
        compiler_params=pltpu.CompilerParams(
            collective_id=0, has_side_effects=True, vmem_limit_bytes=20 * 2**20
        ),
        cost_estimate=pl.CostEstimate(flops=2 * 10**10, bytes_accessed=8 * 10**7, transcendentals=0),
        name="states",
    )(keys, values, conv_weight)
    nb = 640
    once = lambda shape: pl.BlockSpec(shape, lambda i, ts: (0,) * len(shape), pipeline_mode=pl.Buffered(1))
    update, fresh, total = pl.pallas_call(
        functools.partial(project_kernel, float(tokens * n)),
        out_shape=(
            jax.ShapeDtypeStruct((2, width, tokens), F32),
            jax.ShapeDtypeStruct((NH, HD, HD), F32),
            jax.ShapeDtypeStruct((NH, HD), F32),
        ),
        grid_spec=pltpu.PrefetchScalarGridSpec(
            num_scalar_prefetch=1,
            grid=(pl.cdiv(width, nb),),
            in_specs=[
                once((2, CH, tokens)),
                once((3, NR * 8, NC * LT)),
                once((2, CH, tokens)),
                pl.BlockSpec((gate_table.shape[0], nb), lambda i, ts: (0, i)),
                pl.BlockSpec((CH, nb), lambda i, ts: (0, i)),
            ],
            out_specs=(
                pl.BlockSpec((2, nb, tokens), lambda i, ts: (0, i, 0)),
                pl.BlockSpec((NH, HD, HD), lambda i, ts: (0, 0, 0)),
                pl.BlockSpec((NH, HD), lambda i, ts: (0, 0)),
            ),
            scratch_shapes=[
                pltpu.VMEM((CH, 2 * tokens), BF16),
                pltpu.VMEM((640, 256), F32),
                pltpu.VMEM((LT, nb), F32),
            ],
        ),
        compiler_params=pltpu.CompilerParams(
            dimension_semantics=("arbitrary",), vmem_limit_bytes=28 * 2**20
        ),
        name="project",
    )(timesteps, queries, states, conv, gate_table, out_weight)
    return jnp.swapaxes(update, 1, 2), fresh, total


def solution(mesh):
    n = mesh.shape["tm"]
    placed = (
        P(None, ("grp", "tm"), None),
        P(None, ("grp", "tm"), None),
        P(None, ("grp", "tm"), None),
        P("grp"),
        P(),
        P(),
        P(),
    )
    return jax.shard_map(
        functools.partial(local, n),
        mesh=mesh,
        in_specs=placed,
        out_specs=(P(None, ("grp", "tm"), None), P("grp", None, None), P("grp", None)),
        check_vma=False,
    )
```

```python
import functools

import jax
import jax.numpy as jnp
from jax import lax
from jax.experimental import pallas as pl
from jax.experimental.pallas import tpu as pltpu
from jax.sharding import PartitionSpec as P

NH = 16
HD = 70
COLS = 64
CH = NH * HD
LT = 128
NC = -(-CH // LT)
NR = 9
TILES = NR * NC - 1
SPARE = NC * LT - CH
EDGE = LT - SPARE
MESH = pl.DeviceIdType.MESH
F32 = jnp.float32
BF16 = jnp.bfloat16


def spans(width):
    out = []
    for c0 in range(0, CH, width):
        c1 = min(c0 + width, CH)
        h0, h1 = c0 // HD, (c1 - 1) // HD
        r0 = h0 * HD // LT * LT
        r1 = min(-(-(h1 + 1) * HD // LT) * LT, CH)
        out.append((c0, c1, h0, h1, r0, r1))
    return out


def local_state(k_ref, v_ref, s, part, band, put):
    ones = jnp.ones((8, k_ref.shape[2]), BF16)
    lanes = (((1,), (1,)), ((), ()))
    for c, (c0, c1, h0, h1, r0, r1) in enumerate(spans(LT)):
        w = c1 - c0
        band[0 : r1 - r0, 0:w] = lax.dot_general(
            k_ref[s, r0:r1, :], v_ref[s, c0:c1, :], lanes, preferred_element_type=F32
        )
        count = lax.dot_general(ones, k_ref[s, c0:c1, :], lanes, preferred_element_type=F32)[0:1]
        lane = c0 + lax.broadcasted_iota(jnp.int32, (NR * 8, w), 1)
        row = lax.broadcasted_iota(jnp.int32, (NR * 8, w), 0)
        tile = jnp.zeros((NR * 8, w), F32)
        for h in range(h0, h1 + 1):
            rows = band[h * HD - r0 : h * HD - r0 + NR * 8, 0:w]
            tile = jnp.where((lane >= h * HD) & (lane < (h + 1) * HD), rows, tile)
        tile = jnp.where(row < HD, tile, jnp.where(row == HD, count, 0.0))
        for r in range(NR - (c == NC - 1)):
            put(part, s, r * NC + c, slice(0, w), tile[8 * r : 8 * r + 8])
        if c == NC - 1:
            for i in range(EDGE // SPARE):
                piece = tile[8 * NR - 8 :, SPARE * i : SPARE * i + SPARE]
                put(part, s, i * NC + c, slice(EDGE, LT), piece)


def pack(v_ref, lower, out_ref):
    base = v_ref.shape[2] - LT if lower else 0
    lane = lax.broadcasted_iota(jnp.int32, (CH // 2, LT), 1)
    one = v_ref[0, 0 : CH // 2, base : base + LT].astype(F32)
    two = pltpu.roll(v_ref[0, CH // 2 : CH, base : base + LT].astype(F32), LT // 2, 1)
    keep = lane >= LT // 2 if lower else lane < LT // 2
    out_ref[...] = jnp.where(keep, one, two).astype(BF16)


def unpack(rim_ref, rims):
    lane_block = rim_ref[...].astype(F32)
    rims[0 : CH // 2] = pltpu.roll(lane_block, LT // 2, 1)
    rims[CH // 2 : CH] = lane_block


def convolve(v_ref, s, above, below, taps, out_ref):
    tokens = v_ref.shape[2]
    step = CH // 10
    lane = lax.broadcasted_iota(jnp.int32, (step, tokens), 1)
    col = lane % COLS
    for c0 in range(0, CH, step):
        mid = v_ref[s, c0 : c0 + step, :].astype(F32)
        top = above[c0 : c0 + step, :]
        low = below[c0 : c0 + step, :]
        blank = jnp.zeros((step, tokens - LT), F32)
        rows = (
            jnp.where(lane < COLS, jnp.concatenate([top, blank], axis=1), pltpu.roll(mid, COLS, 1)),
            mid,
            jnp.where(
                lane >= tokens - COLS, jnp.concatenate([blank, low], axis=1), pltpu.roll(mid, tokens - COLS, 1)
            ),
        )
        acc = None
        for b in range(3):
            one = sum(rows[a] * taps[c0 : c0 + step, 3 * a + b : 3 * a + b + 1] for a in range(3))
            if b == 0:
                one = jnp.where(col != 0, pltpu.roll(one, 1, 1), 0.0)
            if b == 2:
                one = jnp.where(col != COLS - 1, pltpu.roll(one, tokens - 1, 1), 0.0)
            acc = one if acc is None else acc + one
        out_ref[s, c0 : c0 + step, :] = acc


def gather_kernel(
    n, m, k_hbm, v_hbm, cw_ref, st_ref, conv_ref,
    k_ref, v_ref, in_sem,
    part, cin, cur, rin, full, edge, rim, above, below, wide, taps, band,
    core_s, core_r, p1_s, p1_r, p2_s, p2_r, fw_s, fw_r, rim_s, rim_r,
):
    me = lax.axis_index("tm")
    half = n // 2
    core = me % 2
    chip = me // 2
    mate = chip * 2 + (1 - core)

    def at(k):
        return lax.rem(chip + k, half) * 2 + core

    def place(idx):
        g, j = idx // m, idx % m
        return g // half, g % half, j

    def put(ref, s, idx, lanes, value):
        c, p, j = place(idx)
        ref[s, c, p, j, :, lanes] = value

    def fetch(i, s):
        src, dst = ((k_hbm, k_ref), (v_hbm, v_ref))[i]
        return pltpu.make_async_copy(src.at[s], dst.at[s], in_sem.at[i, s])

    for s in range(2):
        for i in range(2):
            fetch(i, s).start()
    barrier = pltpu.get_barrier_semaphore()
    pl.semaphore_signal(barrier, inc=1, device_id={"tm": mate}, device_id_type=MESH)
    for k in range(1, half):
        pl.semaphore_signal(barrier, inc=1, device_id={"tm": at(k)}, device_id_type=MESH)
    beside = lax.rem(me + 2 * core - 1 + n, n)
    pl.semaphore_signal(barrier, inc=1, device_id={"tm": beside}, device_id_type=MESH)
    pl.semaphore_wait(barrier, half + 1)

    def remote(src, dst, ss, rs, dev):
        return pltpu.make_async_remote_copy(
            src_ref=src, dst_ref=dst, send_sem=ss, recv_sem=rs, device_id={"tm": dev}, device_id_type=MESH
        )

    def swap(s):
        return remote(part.at[s, 1 - core], cin.at[s], core_s.at[s], core_r.at[s], mate)

    def first(s, k):
        return remote(cur.at[s, lax.rem(chip + k, half)], rin.at[s, k], p1_s.at[s, k], p1_r.at[s, k], at(k))

    def second(s, k):
        return remote(
            full.at[s, core, chip], full.at[s, core, chip], p2_s.at[s, k], p2_r.at[s, k], at(k)
        )

    def second_in(s, k):
        src = lax.rem(chip + half - k, half)
        return remote(full.at[s, core, src], full.at[s, core, src], p2_s.at[s, k], p2_r.at[s, k], at(k))

    def onward(s, k):
        src = lax.rem(chip + half - k, half)
        return remote(full.at[s, core, src], full.at[s, core, src], fw_s.at[s, k], fw_r.at[s, k], mate)

    def onward_in(s, k):
        src = lax.rem(chip + half - k, half)
        return remote(full.at[s, 1 - core, src], full.at[s, 1 - core, src], fw_s.at[s, k], fw_r.at[s, k], mate)

    down = remote(edge.at[0], rim.at[0], rim_s.at[0], rim_r.at[0], me + 1)
    up = remote(edge.at[1], rim.at[1], rim_s.at[1], rim_r.at[1], me - 1)

    part[...] = jnp.zeros_like(part)
    for i in range(2):
        fetch(i, 0).wait()
    local_state(k_ref, v_ref, 0, part, band, put)
    swap(0).start()
    pack(v_ref, True, edge.at[0])
    pack(v_ref, False, edge.at[1])

    @pl.when(me < n - 1)
    def _():
        down.start()

    @pl.when(me > 0)
    def _():
        up.start()

    for i in range(2):
        fetch(i, 1).wait()
    local_state(k_ref, v_ref, 1, part, band, put)
    swap(1).start()
    wide[...] = jnp.zeros_like(wide)
    wide[0:9, 0:CH] = cw_ref[...]
    for c in range(NC):
        taps[LT * c : LT * c + LT, :] = jnp.transpose(wide[:, LT * c : LT * c + LT])
    for s in range(2):
        swap(s).wait()
        cur[s] = part[s, core] + cin[s]
        for k in range(1, half):
            first(s, k).start()

    @pl.when(me == 0)
    def _():
        rim[0] = jnp.zeros_like(rim[0])

    @pl.when(me == n - 1)
    def _():
        rim[1] = jnp.zeros_like(rim[1])

    @pl.when(me < n - 1)
    def _():
        down.wait_send()
        up.wait_recv()

    @pl.when(me > 0)
    def _():
        up.wait_send()
        down.wait_recv()

    unpack(rim.at[0], above)
    unpack(rim.at[1], below)
    for s in range(2):
        convolve(v_ref, s, above, below, taps, conv_ref)
        total = cur[s, chip]
        for k in range(1, half):
            first(s, k).wait()
            total = total + rin[s, k]
        full[s, core, chip] = total
        for k in range(1, half):
            second(s, k).start()
        onward(s, 0).start()
    for s in range(2):
        for k in range(1, half):
            second_in(s, k).wait_recv()
            onward(s, k).start()
        for k in range(1, half):
            second(s, k).wait_send()
    for s in range(2):
        for k in range(half):
            onward(s, k).wait_send()
            onward_in(s, k).wait_recv()
    for idx in range(TILES):
        r, c = idx // NC, idx % NC
        where = place(idx)
        whole = full[(0, *where)]
        moved = whole - part[(0, *where)] + part[(1, *where)]
        for i, tile in enumerate((whole, moved, full[(1, *where)])):
            st_ref[i, 8 * r : 8 * r + 8, LT * c : LT * c + LT] = tile
            if c == NC - 1 and r < EDGE // SPARE:
                lane = LT * c + SPARE * r
                st_ref[i, 8 * NR - 8 :, lane : lane + SPARE] = tile[:, EDGE:]


def split(x):
    high = x.astype(BF16)
    return high, (x - high.astype(F32)).astype(BF16)


def mix(q_ref, st_ref, conv_ref, s, mixed, block):
    tokens = q_ref.shape[2]
    firsts = (((0,), (0,)), ((), ()))
    for c0, c1, h0, h1, r0, r1 in spans(256):
        w, depth = c1 - c0, r1 - r0
        block[...] = jnp.zeros_like(block)
        state = st_ref[s, 0:72, c0:c1]
        lane = c0 + lax.broadcasted_iota(jnp.int32, (HD, w), 1)
        for h in range(h0, h1 + 1):
            block[h * HD - r0 : (h + 1) * HD - r0, 0:w] = jnp.where(
                (lane >= h * HD) & (lane < (h + 1) * HD), state[0:HD], 0.0
            )
        query = q_ref[s, r0:r1, :]
        numer = sum(
            lax.dot_general(x, query, firsts, preferred_element_type=F32) for x in split(block[0:depth, 0:w])
        )
        row_head = jnp.floor((lax.broadcasted_iota(jnp.int32, (w, depth), 0).astype(F32) + (c0 + 0.5)) / HD)
        col_head = jnp.floor((lax.broadcasted_iota(jnp.int32, (w, depth), 1).astype(F32) + (r0 + 0.5)) / HD)
        norm = jnp.where(row_head == col_head, st_ref[s, HD : HD + 1, r0:r1], 0.0)
        denom = sum(jnp.dot(x, query, preferred_element_type=F32) for x in split(norm))
        mixed[c0:c1, s * tokens : (s + 1) * tokens] = (numer / denom + conv_ref[s, c0:c1, :]).astype(BF16)


def project_kernel(
    total_tokens, ts_ref, q_ref, st_ref, conv_ref, gate_ref, w_ref, out_ref, fs_ref, ft_ref, mixed, block, gates
):
    tokens = q_ref.shape[2]

    @pl.when(pl.program_id(0) == 0)
    def _():
        for s in range(2):
            mix(q_ref, st_ref, conv_ref, s, mixed, block)
        for h in range(NH):
            base = min(h * HD // LT * LT, NC * LT - 2 * LT)
            both = st_ref[2, :, base : base + 2 * LT] / total_tokens
            both = pltpu.roll(both, (2 * LT - (h * HD - base)) % (2 * LT), 1)
            fs_ref[h] = both[0:HD, 0:HD]
            ft_ref[h : h + 1, :] = both[HD : HD + 1, 0:HD]

    for s in range(2):
        gates[s : s + 1, :] = gate_ref[pl.ds(ts_ref[s], 1), :]
    acc = lax.dot_general(w_ref[...], mixed[...], (((0,), (0,)), ((), ())), preferred_element_type=F32)
    for c in range(0, acc.shape[0], LT):
        gate = jnp.transpose(gates[:, c : c + LT])
        for s in range(2):
            out_ref[s, c : c + LT, :] = gate[:, s : s + 1] * acc[c : c + LT, s * tokens : (s + 1) * tokens]


def local(n, queries, keys, values, timesteps, gate_table, out_weight, conv_weight):
    tokens = queries.shape[1]
    width = out_weight.shape[1]
    half = n // 2
    queries, keys, values = (jnp.swapaxes(x, 1, 2) for x in (queries, keys, values))
    m = -(-TILES // n)
    vmem = pl.BlockSpec(memory_space=pltpu.VMEM)
    dma = pltpu.SemaphoreType.DMA
    states, conv = pl.pallas_call(
        functools.partial(gather_kernel, n, m),
        out_shape=(
            jax.ShapeDtypeStruct((3, NR * 8, NC * LT), F32),
            jax.ShapeDtypeStruct((2, CH, tokens), F32),
        ),
        in_specs=[pl.BlockSpec(memory_space=pltpu.MemorySpace.HBM)] * 2 + [vmem],
        out_specs=(vmem, vmem),
        scratch_shapes=[
            pltpu.VMEM((2, CH, tokens), BF16),
            pltpu.VMEM((2, CH, tokens), BF16),
            dma((2, 2)),
            pltpu.VMEM((2, 2, half, m, 8, LT), F32),
            pltpu.VMEM((2, half, m, 8, LT), F32),
            pltpu.VMEM((2, half, m, 8, LT), F32),
            pltpu.VMEM((2, half, m, 8, LT), F32),
            pltpu.VMEM((2, 2, half, m, 8, LT), F32),
            pltpu.VMEM((2, CH // 2, LT), BF16),
            pltpu.VMEM((2, CH // 2, LT), BF16),
            pltpu.VMEM((CH, LT), F32),
            pltpu.VMEM((CH, LT), F32),
            pltpu.VMEM((LT, NC * LT), F32),
            pltpu.VMEM((NC * LT, LT), F32),
            pltpu.VMEM((640, LT), F32),
            dma((2,)), dma((2,)),
            dma((2, half)), dma((2, half)),
            dma((2, half)), dma((2, half)),
            dma((2, half)), dma((2, half)),
            dma((2,)), dma((2,)),
        ],
        compiler_params=pltpu.CompilerParams(
            collective_id=0, has_side_effects=True, vmem_limit_bytes=20 * 2**20
        ),
        cost_estimate=pl.CostEstimate(flops=2 * 10**10, bytes_accessed=8 * 10**7, transcendentals=0),
        name="states",
    )(keys, values, conv_weight)
    nb = 640
    once = lambda shape: pl.BlockSpec(shape, lambda i, ts: (0,) * len(shape), pipeline_mode=pl.Buffered(1))
    update, fresh, total = pl.pallas_call(
        functools.partial(project_kernel, float(tokens * n)),
        out_shape=(
            jax.ShapeDtypeStruct((2, width, tokens), F32),
            jax.ShapeDtypeStruct((NH, HD, HD), F32),
            jax.ShapeDtypeStruct((NH, HD), F32),
        ),
        grid_spec=pltpu.PrefetchScalarGridSpec(
            num_scalar_prefetch=1,
            grid=(pl.cdiv(width, nb),),
            in_specs=[
                once((2, CH, tokens)),
                once((3, NR * 8, NC * LT)),
                once((2, CH, tokens)),
                pl.BlockSpec((gate_table.shape[0], nb), lambda i, ts: (0, i)),
                pl.BlockSpec((CH, nb), lambda i, ts: (0, i)),
            ],
            out_specs=(
                pl.BlockSpec((2, nb, tokens), lambda i, ts: (0, i, 0)),
                pl.BlockSpec((NH, HD, HD), lambda i, ts: (0, 0, 0)),
                pl.BlockSpec((NH, HD), lambda i, ts: (0, 0)),
            ),
            scratch_shapes=[
                pltpu.VMEM((CH, 2 * tokens), BF16),
                pltpu.VMEM((640, 256), F32),
                pltpu.VMEM((LT, nb), F32),
            ],
        ),
        compiler_params=pltpu.CompilerParams(
            dimension_semantics=("arbitrary",), vmem_limit_bytes=28 * 2**20
        ),
        name="project",
    )(timesteps, queries, states, conv, gate_table, out_weight)
    return jnp.swapaxes(update, 1, 2), fresh, total


def solution(mesh):
    n = mesh.shape["tm"]
    placed = (
        P(None, ("grp", "tm"), None),
        P(None, ("grp", "tm"), None),
        P(None, ("grp", "tm"), None),
        P("grp"),
        P(),
        P(),
        P(),
    )
    return jax.shard_map(
        functools.partial(local, n),
        mesh=mesh,
        in_specs=placed,
        out_specs=(P(None, ("grp", "tm"), None), P("grp", None, None), P("grp", None)),
        check_vma=False,
    )
```
